32 devices in a mesh: vid: 2 (over x), tm: 16 (over z, y, core).
Axes of the slice: x: 2, y: 2, z: 4, core: 2. Of those that a mesh axis runs over, the one named last changes fastest.
Arguments:
- queries: bfloat16 [4096, 1536], P(('vid', 'tm')), parts along dimension 0, may hold values from -6 to 6
- keys: bfloat16 [4096, 1536], P(('vid', 'tm')), parts along dimension 0, may hold values from -6 to 6
- values: bfloat16 [4096, 1536], P(('vid', 'tm')), parts along dimension 0, may hold values from -6 to 6
- far_picks: int32 [64, 8], P(('vid', 'tm')), parts along dimension 0, may hold values from 0 to 1
- out_weight: bfloat16 [1536, 1536], replicated, may hold values from -0.15625 to 0.15625
Outputs:
- mixed: bfloat16 [4096, 1536], P(('vid', 'tm')), parts along dimension 0
The draws below stay inside these ranges and needn't reach their ends.
There are 2 independent parts, one for each index of `vid`. The reference program is written for one: setup_inputs(seed, part) draws one part's arguments, and reference() takes and returns one part's arrays. A program takes and returns all parts, laid end to end along the dimension named above; an argument that names none is the same for every part. Nothing has to cross between parts.
All inputs are finite; a program needn't handle non-finite values.
Results may differ from the reference program's by a relative error of at most 0.0056.
Values may be sent and summed in bfloat16 or wider, within the bound.
A program may use at most 64 MiB of HBM per device.

```python
import jax
import jax.numpy as jnp
from jax import lax

D = 1536
HEADS = 12
HEAD_DIM = 128
BLK = 64
LEVELS = 2
PICKS = 2
TOK_DEV = 128
FAR = 8
NB_DEV = 2
TOKENS = 2048
N_TM = 16


def paired_draw(key):
    base_key = jax.random.fold_in(key, 101)
    first_key, second_key = jax.random.split(base_key, 2)
    full_shape = (TOKENS, D)
    query_raw = jnp.clip(jax.random.normal(first_key, full_shape, jnp.float32), -5.0, 5.0)
    key_raw = jnp.clip(jax.random.normal(second_key, full_shape, jnp.float32), -5.0, 5.0)
    return (jnp.clip(query_raw, -6.0, 6.0), jnp.clip(key_raw, -6.0, 6.0))


def draw_queries(key, part):
    return paired_draw(key)[0].astype(jnp.bfloat16)


def draw_keys(key, part):
    return paired_draw(key)[1].astype(jnp.bfloat16)


def place_ends(drawn, own_key, low, high):
    longest = drawn.shape.index(max(drawn.shape))
    spots = []
    for shift in (0, 1):
        where = [jax.random.randint(jax.random.fold_in(own_key, axis), (), 0, length) for axis, length in enumerate(drawn.shape)]
        where[longest] = (where[longest] + shift) % drawn.shape[longest]
        spots.append(tuple(where))
    return drawn.at[spots[0]].set(low).at[spots[1]].set(high)


def levels(key, extent, cuts, smallest, largest):
    level = 1.0
    for axis_at, parts in cuts:
        draws = jax.random.uniform(jax.random.fold_in(jax.random.fold_in(key, 6), axis_at), (parts,), jnp.float32, smallest / len(cuts), largest / len(cuts))
        level = level * jnp.repeat(jnp.exp(draws), extent[axis_at] // parts).reshape((-1,) + (1,) * (len(extent) - 1 - axis_at))
    return level


def centred(key, extent, scale, reach, cuts=(), kind=jnp.bfloat16):
    drawn = scale * jax.random.normal(key, extent, jnp.float32)
    if cuts:
        drawn = drawn * levels(key, extent, cuts, -0.22, 0.18)
    return jnp.clip(drawn, -reach, reach).astype(kind)


def setup_inputs(seed: int = 0, part: int = 0) -> dict:
    key_of = jax.random.split(jax.random.key(seed), 6)
    own_keys = jax.random.split(jax.random.fold_in(key_of[5], part), 6)
    queries = draw_queries(jax.random.fold_in(jax.random.fold_in(key_of[5], part), 71), part)
    keys = draw_keys(jax.random.fold_in(jax.random.fold_in(key_of[5], part), 71), part)
    values = centred(own_keys[2], (TOKENS, D), 1.0, 6.0, ((0, 16),))
    far_picks = place_ends(jax.random.randint(own_keys[3], (TOKENS // BLK, FAR), 0, NB_DEV), jax.random.fold_in(own_keys[3], 1), 0, NB_DEV - 1).astype(jnp.int32)
    out_weight = centred(key_of[4], (D, D), D ** -0.5, 0.15625)
    return {"queries": queries, "keys": keys, "values": values, "far_picks": far_picks, "out_weight": out_weight}


def far_offsets():
    offset_list = []
    for column in range(FAR):
        magnitude = 2 ** (1 + (column // PICKS) % LEVELS)
        offset_list.append(-magnitude if column < FAR // 2 else magnitude)
    return offset_list


def attend(query_rows, near_pair, near_valid, far_pair, far_valid, out_weight):
    blocks = query_rows.shape[0] // BLK
    scale = HEAD_DIM ** -0.5
    query_heads = query_rows.reshape(blocks, BLK, HEADS, HEAD_DIM).astype(jnp.float32)
    near_keys = near_pair[0].reshape(-1, HEADS, HEAD_DIM).astype(jnp.float32)
    near_values = near_pair[1].reshape(-1, HEADS, HEAD_DIM).astype(jnp.float32)
    far_keys = far_pair[0].reshape(blocks, -1, HEADS, HEAD_DIM).astype(jnp.float32)
    far_values = far_pair[1].reshape(blocks, -1, HEADS, HEAD_DIM).astype(jnp.float32)
    near_scores = jnp.einsum("bqhd,khd->bhqk", query_heads, near_keys) * scale
    near_scores = jnp.where(near_valid, near_scores, jnp.float32(-1e30))
    far_scores = jnp.einsum("bqhd,bkhd->bhqk", query_heads, far_keys) * scale
    far_scores = jnp.where(far_valid, far_scores, jnp.float32(-1e30))
    top_score = jnp.maximum(jnp.max(near_scores, -1), jnp.max(far_scores, -1))[..., None]
    near_exp = jnp.exp(near_scores - top_score)
    far_exp = jnp.exp(far_scores - top_score)
    total = jnp.sum(near_exp, -1) + jnp.sum(far_exp, -1)
    near_weights = lax.optimization_barrier(near_exp.astype(jnp.bfloat16)).astype(jnp.float32)
    far_weights = lax.optimization_barrier(far_exp.astype(jnp.bfloat16)).astype(jnp.float32)
    summed = jnp.einsum("bhqk,khd->bqhd", near_weights, near_values)
    summed = summed + jnp.einsum("bhqk,bkhd->bqhd", far_weights, far_values)
    attended = (summed / jnp.transpose(total, (0, 2, 1))[..., None]).reshape(blocks * BLK, D).astype(jnp.bfloat16)
    return jnp.dot(attended, out_weight, preferred_element_type=jnp.float32).astype(jnp.bfloat16)


def reference(queries, keys, values, far_picks, out_weight):
    blocks = TOK_DEV // BLK
    pair = jnp.stack([keys, values])
    padded = jnp.pad(pair, ((0, 0), (TOK_DEV, TOK_DEV), (0, 0)))
    offset_list = far_offsets()

    def one_device(device):
        start = (device * TOK_DEV).astype(jnp.int32)
        query_rows = lax.dynamic_slice_in_dim(queries, start, TOK_DEV, 0)
        near_pair = lax.dynamic_slice_in_dim(padded, start, 3 * TOK_DEV, 1)
        picks = lax.dynamic_slice_in_dim(far_picks, (device * blocks).astype(jnp.int32), blocks, 0)
        chosen_list = []
        valid_list = []
        for column in range(FAR):
            source = device + offset_list[column]
            usable = (source >= 0) & (source < N_TM)
            source_start = (jnp.clip(source, 0, N_TM - 1) * TOK_DEV).astype(jnp.int32)
            shard = lax.dynamic_slice_in_dim(pair, source_start, TOK_DEV, 1).reshape(2, blocks, BLK, D)
            chosen_list.append(jnp.take(shard, picks[:, column], axis=1))
            valid_list.append(usable)
        far_pair = jnp.stack(chosen_list, 2).reshape(2, blocks, FAR * BLK, D)
        far_valid = jnp.repeat(jnp.stack(valid_list), BLK)
        near_valid = jnp.repeat(jnp.stack([device > 0, jnp.array(True), device < N_TM - 1]), TOK_DEV)
        return attend(query_rows, near_pair, near_valid, far_pair, far_valid, out_weight)

    result = lax.map(one_device, jnp.arange(N_TM, dtype=jnp.int32))
    return result.reshape(TOKENS, D)
```

```python
import functools
import math

import jax
import jax.numpy as jnp
from jax import lax
from jax.experimental import pallas as pl
from jax.experimental.pallas import tpu as pltpu
from jax.sharding import PartitionSpec as P

HEADS = 12
HEAD_DIM = 128
BLK = 64
NEG = -1e30
EXP_SCALE = HEAD_DIM ** (-0.5) * math.log2(math.e)
OWN, SIB, YN, ZP, ZM, DG, XF = range(7)
MESH = pl.DeviceIdType.MESH


def kernel(
    devices,
    picks,
    q_hbm,
    k_hbm,
    v_hbm,
    out,
    qv,
    kbuf,
    vbuf,
    mult,
    top,
    tot,
    acc,
    load_sem,
    send_sem,
    recv_sem,
):
    rows = q_hbm.shape[0]
    half = rows // 2
    chips = devices // 2
    p = lax.axis_index("tm")
    chip = p // 2
    core = p % 2
    even = chip % 2 == 0
    step = jnp.where(even, 1, -1)
    has_p = (chip + 2 * step >= 0) & (chip + 2 * step < chips)
    has_m = (chip - 2 * step >= 0) & (chip - 2 * step < chips)
    gives_y = (core + chip) % 2 == 0
    gives_d = jnp.logical_not(gives_y)

    sib = p + 1 - 2 * core
    y_dev = p + 2 * step
    zp_dev = p + 4 * step
    zm_dev = p - 4 * step

    def slot(buf, index):
        return buf.at[pl.ds(index * rows, rows)]

    def part(buf, index, which):
        return buf.at[pl.ds(index * rows + which * half, half)]

    def remote(src, dst, number, kv, dev):
        return pltpu.make_async_remote_copy(
            src_ref=src,
            dst_ref=dst,
            send_sem=send_sem.at[number, kv],
            recv_sem=recv_sem.at[number, kv],
            device_id={"tm": dev},
            device_id_type=MESH,
        )

    bufs = (kbuf, vbuf)
    hbms = (k_hbm, v_hbm)

    def to_sib(kv):
        return remote(hbms[kv], slot(bufs[kv], SIB), 0, kv, sib)

    def to_y(kv):
        return remote(hbms[kv], slot(bufs[kv], YN), 1, kv, y_dev)

    def to_zp(kv):
        return remote(hbms[kv], slot(bufs[kv], ZM), 2, kv, zp_dev)

    def to_zm(kv):
        return remote(hbms[kv], slot(bufs[kv], ZP), 3, kv, zm_dev)

    def relay_y(kv):
        return remote(part(bufs[kv], YN, 0), part(bufs[kv], DG, 0), 4, kv, zp_dev)

    def relay_z(kv):
        return remote(part(bufs[kv], ZP, 1), part(bufs[kv], DG, 1), 5, kv, y_dev)

    def hand_y(kv):
        return remote(slot(bufs[kv], YN), slot(bufs[kv], XF), 6, kv, sib)

    def hand_d(kv):
        return remote(slot(bufs[kv], DG), slot(bufs[kv], XF), 6, kv, sib)

    loads = [
        pltpu.make_async_copy(q_hbm, qv, load_sem.at[0]),
        pltpu.make_async_copy(k_hbm, slot(kbuf, OWN), load_sem.at[1]),
        pltpu.make_async_copy(v_hbm, slot(vbuf, OWN), load_sem.at[2]),
    ]
    for load in loads:
        load.start()

    barrier = pltpu.get_barrier_semaphore()

    def greet(dev):
        pl.semaphore_signal(barrier, inc=1, device_id={"tm": dev}, device_id_type=MESH)

    greet(sib)
    greet(y_dev)

    @pl.when(has_p)
    def _():
        greet(zp_dev)

    @pl.when(has_m)
    def _():
        greet(zm_dev)

    pl.semaphore_wait(barrier, 2 + jnp.where(has_p, 1, 0) + jnp.where(has_m, 1, 0))

    for kv in range(2):
        to_y(kv).start()

        @pl.when(has_p)
        def _():
            to_zp(kv).start()

        @pl.when(has_m)
        def _():
            to_zm(kv).start()

        to_sib(kv).start()

    ints = jnp.int32
    row_first = lax.broadcasted_iota(ints, (rows, rows), 0) < BLK
    col_first = lax.broadcasted_iota(ints, (rows, rows), 1) < BLK

    def fill(index, up, down, valid):
        one = jnp.where(valid, 1, 0)
        seconds = [
            jnp.where(even, picks[b, up] + picks[b, up + 1], picks[b, down] + picks[b, down + 1])
            for b in range(2)
        ]
        cells = [[((2 - n) * one).astype(jnp.float32), (n * one).astype(jnp.float32)] for n in seconds]
        mult[index] = jnp.where(
            row_first,
            jnp.where(col_first, cells[0][0], cells[0][1]),
            jnp.where(col_first, cells[1][0], cells[1][1]),
        )

    fill(0, 4, 0, True)
    fill(1, 6, 2, has_p)
    fill(2, 2, 6, has_m)
    fill(3, 0, 4, has_m)
    x_valid = gives_d | has_m
    mult[4] = jnp.full((rows, rows), jnp.where(x_valid, 1.0, 0.0), jnp.float32)

    @pl.when(jnp.logical_not(has_p))
    def _():
        vbuf[ZP * rows : (ZP + 1) * rows] = jnp.zeros((rows, vbuf.shape[1]), vbuf.dtype)

    @pl.when(jnp.logical_not(has_m))
    def _():
        vbuf[ZM * rows : (DG + 1) * rows] = jnp.zeros((2 * rows, vbuf.shape[1]), vbuf.dtype)

    @pl.when(jnp.logical_not(x_valid))
    def _():
        vbuf[XF * rows : (XF + 1) * rows] = jnp.zeros((rows, vbuf.shape[1]), vbuf.dtype)

    def head_group(head, first_slot, factors, first, last):
        columns = pl.ds(pl.multiple_of(head * HEAD_DIM, HEAD_DIM), HEAD_DIM)
        count = len(factors)
        slots = pl.ds(first_slot * rows, count * rows)
        scores = lax.dot_general(
            qv[:, columns],
            kbuf[slots, columns],
            (((1,), (1,)), ((), ())),
            preferred_element_type=jnp.float32,
        )
        pieces = []
        for i, factor in enumerate(factors):
            piece = scores[:, i * rows : (i + 1) * rows]
            if factor is not None:
                piece = jnp.where(mult[factor] > 0, piece, NEG)
            pieces.append(piece)
        high = functools.reduce(jnp.maximum, pieces)
        high = jnp.broadcast_to(jnp.max(high, axis=1, keepdims=True), high.shape)
        if not first:
            before = top[head]
            high = jnp.maximum(high, before)
            fade = jnp.exp2((before - high) * EXP_SCALE)
        weights = []
        for piece, factor in zip(pieces, factors):
            weight = jnp.exp2((piece - high) * EXP_SCALE)
            if factor is not None:
                weight = weight * mult[factor]
            weights.append(weight)
        summed = functools.reduce(jnp.add, weights)
        summed = jnp.broadcast_to(jnp.sum(summed, axis=1, keepdims=True), summed.shape)
        mixed = jnp.dot(
            jnp.concatenate([w.astype(jnp.bfloat16) for w in weights], axis=1),
            vbuf[slots, columns],
            preferred_element_type=jnp.float32,
        )
        if not first:
            summed = summed + tot[head] * fade
            mixed = mixed + acc[head] * fade
        if last:
            out[:, columns] = (mixed / summed).astype(out.dtype)
        else:
            top[head] = high
            tot[head] = summed
            acc[head] = mixed

    def group(first_slot, factors, first, last, unroll):
        def body(index, carry):
            for u in range(unroll):
                head_group(index * unroll + u, first_slot, factors, first, last)
            return carry

        if unroll == HEADS:
            body(0, 0)
        else:
            lax.fori_loop(0, HEADS // unroll, body, 0)

    for load in loads:
        load.wait()
    for kv in range(2):
        to_sib(kv).wait_recv()
    group(OWN, (None, None), True, False, 4)

    for kv in range(2):
        to_y(kv).wait_recv()

        @pl.when(has_p)
        def _():
            relay_y(kv).start()

        @pl.when(gives_y)
        def _():
            hand_y(kv).start()

        @pl.when(has_p)
        def _():
            to_zm(kv).wait_recv()
            relay_z(kv).start()

    @pl.when(has_m)
    def _():
        for kv in range(2):
            to_zp(kv).wait_recv()

    group(YN, (0, 1, 2), False, False, 4)

    for kv in range(2):

        @pl.when(has_m)
        def _():
            relay_y(kv).wait_recv()
            relay_z(kv).wait_recv()

        @pl.when(has_m & gives_d)
        def _():
            hand_d(kv).start()

    for kv in range(2):

        @pl.when(x_valid)
        def _():
            hand_y(kv).wait_recv()

    group(DG, (3, 4), False, True, 4)

    for kv in range(2):
        to_sib(kv).wait_send()
        to_y(kv).wait_send()

        @pl.when(has_p)
        def _():
            to_zp(kv).wait_send()
            relay_y(kv).wait_send()
            relay_z(kv).wait_send()

        @pl.when(has_m)
        def _():
            to_zm(kv).wait_send()

        @pl.when(gives_y | has_m)
        def _():
            hand_y(kv).wait_send()


def attention(devices, queries, keys, values, far_picks):
    rows, width = queries.shape
    anywhere = pl.BlockSpec(memory_space=pl.ANY)
    return pl.pallas_call(
        functools.partial(kernel, devices),
        out_shape=jax.ShapeDtypeStruct((rows, width), jnp.bfloat16),
        in_specs=[pl.BlockSpec(memory_space=pltpu.SMEM), anywhere, anywhere, anywhere],
        out_specs=pl.BlockSpec(memory_space=pltpu.VMEM),
        scratch_shapes=[
            pltpu.VMEM((rows, width), jnp.bfloat16),
            pltpu.VMEM((7 * rows, width), jnp.bfloat16),
            pltpu.VMEM((7 * rows, width), jnp.bfloat16),
            pltpu.VMEM((5, rows, rows), jnp.float32),
            pltpu.VMEM((HEADS, rows, HEAD_DIM), jnp.float32),
            pltpu.VMEM((HEADS, rows, HEAD_DIM), jnp.float32),
            pltpu.VMEM((HEADS, rows, HEAD_DIM), jnp.float32),
            pltpu.SemaphoreType.DMA((3,)),
            pltpu.SemaphoreType.DMA((7, 2)),
            pltpu.SemaphoreType.DMA((7, 2)),
        ],
        compiler_params=pltpu.CompilerParams(
            collective_id=0, has_side_effects=True, vmem_limit_bytes=24 * 1024 * 1024
        ),
        name="relay_attention",
    )(far_picks, queries, keys, values)


def solution(mesh):
    devices = mesh.shape["tm"]

    def body(queries, keys, values, far_picks, out_weight):
        attended = attention(devices, queries, keys, values, far_picks)
        return jnp.dot(attended, out_weight, preferred_element_type=jnp.float32).astype(jnp.bfloat16)

    placed = (
        P(("vid", "tm"), None),
        P(("vid", "tm"), None),
        P(("vid", "tm"), None),
        P(("vid", "tm"), None),
        P(),
    )
    return jax.shard_map(
        body, mesh=mesh, in_specs=placed, out_specs=P(("vid", "tm"), None), check_vma=False
    )
```

```python
import functools
import math

import jax
import jax.numpy as jnp
from jax import lax
from jax.experimental import pallas as pl
from jax.experimental.pallas import tpu as pltpu
from jax.sharding import PartitionSpec as P

HEADS = 12
HEAD_DIM = 128
BLK = 64
NEG = -1e30
EXP_SCALE = HEAD_DIM ** (-0.5) * math.log2(math.e)
OWN, SIB, YN, ZP, ZM, DG, XF = range(7)
MESH = pl.DeviceIdType.MESH


def kernel(
    devices,
    picks_hbm,
    q_hbm,
    k_hbm,
    v_hbm,
    w_hbm,
    out,
    picks,
    qv,
    wv,
    late,
    mixed_heads,
    kbuf,
    vbuf,
    mult,
    top,
    tot,
    acc,
    load_sem,
    send_sem,
    recv_sem,
):
    rows = q_hbm.shape[0]
    half = rows // 2
    chips = devices // 2
    p = lax.axis_index("tm")
    chip = p // 2
    core = p % 2
    even = chip % 2 == 0
    step = jnp.where(even, 1, -1)
    has_p = (chip + 2 * step >= 0) & (chip + 2 * step < chips)
    has_m = (chip - 2 * step >= 0) & (chip - 2 * step < chips)
    gives_y = (core + chip) % 2 == 0
    gives_d = jnp.logical_not(gives_y)

    sib = p + 1 - 2 * core
    y_dev = p + 2 * step
    zp_dev = p + 4 * step
    zm_dev = p - 4 * step

    def slot(buf, index):
        return buf.at[pl.ds(index * rows, rows)]

    def part(buf, index, which):
        return buf.at[pl.ds(index * rows + which * half, half)]

    def remote(src, dst, number, kv, dev):
        return pltpu.make_async_remote_copy(
            src_ref=src,
            dst_ref=dst,
            send_sem=send_sem.at[number, kv],
            recv_sem=recv_sem.at[number, kv],
            device_id={"tm": dev},
            device_id_type=MESH,
        )

    bufs = (kbuf, vbuf)
    hbms = (k_hbm, v_hbm)

    def to_sib(kv):
        return remote(hbms[kv], slot(bufs[kv], SIB), 0, kv, sib)

    def to_y(kv):
        return remote(hbms[kv], slot(bufs[kv], YN), 1, kv, y_dev)

    def to_zp(kv):
        return remote(hbms[kv], slot(bufs[kv], ZM), 2, kv, zp_dev)

    def to_zm(kv):
        return remote(hbms[kv], slot(bufs[kv], ZP), 3, kv, zm_dev)

    def relay_y(kv):
        return remote(part(bufs[kv], YN, 0), part(bufs[kv], DG, 0), 4, kv, zp_dev)

    def relay_z(kv):
        return remote(part(bufs[kv], ZP, 1), part(bufs[kv], DG, 1), 5, kv, y_dev)

    def hand_y(kv, which):
        return remote(part(bufs[kv], YN, which), part(bufs[kv], XF, which), 6 + which, kv, sib)

    def hand_d(kv, which):
        return remote(part(bufs[kv], DG, which), part(bufs[kv], XF, which), 6 + which, kv, sib)

    load_w = pltpu.make_async_copy(w_hbm, wv, load_sem.at[4])
    load_picks = pltpu.make_async_copy(picks_hbm, picks, load_sem.at[3])
    load_picks.start()
    loads = [
        pltpu.make_async_copy(q_hbm, qv, load_sem.at[0]),
        pltpu.make_async_copy(k_hbm, slot(kbuf, OWN), load_sem.at[1]),
        pltpu.make_async_copy(v_hbm, slot(vbuf, OWN), load_sem.at[2]),
    ]
    for load in loads:
        load.start()

    barrier = pltpu.get_barrier_semaphore()

    def greet(dev):
        pl.semaphore_signal(barrier, inc=1, device_id={"tm": dev}, device_id_type=MESH)

    greet(sib)
    greet(y_dev)

    @pl.when(has_p)
    def _():
        greet(zp_dev)

    @pl.when(has_m)
    def _():
        greet(zm_dev)

    pl.semaphore_wait(barrier, 2 + jnp.where(has_p, 1, 0) + jnp.where(has_m, 1, 0))

    for kv in range(2):
        to_y(kv).start()

        @pl.when(has_p)
        def _():
            to_zp(kv).start()

        @pl.when(has_m)
        def _():
            to_zm(kv).start()

        to_sib(kv).start()

    load_w.start()
    load_picks.wait()

    ints = jnp.int32
    row_first = lax.broadcasted_iota(ints, (rows, rows), 0) < BLK
    col_first = lax.broadcasted_iota(ints, (rows, rows), 1) < BLK

    def fill(index, up, down, valid):
        one = jnp.where(valid, 1, 0)
        seconds = [
            jnp.where(even, picks[b, up] + picks[b, up + 1], picks[b, down] + picks[b, down + 1])
            for b in range(2)
        ]
        cells = [[((2 - n) * one).astype(jnp.float32), (n * one).astype(jnp.float32)] for n in seconds]
        mult[index] = jnp.where(
            row_first,
            jnp.where(col_first, cells[0][0], cells[0][1]),
            jnp.where(col_first, cells[1][0], cells[1][1]),
        )

    fill(0, 4, 0, True)
    fill(1, 6, 2, has_p)
    fill(2, 2, 6, has_m)
    fill(3, 0, 4, has_m)
    x_valid = gives_d | has_m
    mult[4] = jnp.full((rows, rows), jnp.where(x_valid, 1.0, 0.0), jnp.float32)

    @pl.when(jnp.logical_not(has_p))
    def _():
        vbuf[ZP * rows : (ZP + 1) * rows] = jnp.zeros((rows, vbuf.shape[1]), vbuf.dtype)

    @pl.when(jnp.logical_not(has_m))
    def _():
        vbuf[ZM * rows : (DG + 1) * rows] = jnp.zeros((2 * rows, vbuf.shape[1]), vbuf.dtype)

    @pl.when(jnp.logical_not(x_valid))
    def _():
        vbuf[XF * rows : (XF + 1) * rows] = jnp.zeros((rows, vbuf.shape[1]), vbuf.dtype)

    def head_group(head, first_slot, factors, first, values_later):
        columns = pl.ds(pl.multiple_of(head * HEAD_DIM, HEAD_DIM), HEAD_DIM)
        count = len(factors)
        slots = pl.ds(first_slot * rows, count * rows)
        scores = lax.dot_general(
            qv[:, columns],
            kbuf[slots, columns],
            (((1,), (1,)), ((), ())),
            preferred_element_type=jnp.float32,
        )
        pieces = []
        for i, factor in enumerate(factors):
            piece = scores[:, i * rows : (i + 1) * rows]
            if factor is not None:
                piece = jnp.where(mult[factor] > 0, piece, NEG)
            pieces.append(piece)
        high = functools.reduce(jnp.maximum, pieces)
        high = jnp.broadcast_to(jnp.max(high, axis=1, keepdims=True), high.shape)
        if not first:
            before = top[head]
            high = jnp.maximum(high, before)
            fade = jnp.exp2((before - high) * EXP_SCALE)
        weights = []
        for piece, factor in zip(pieces, factors):
            weight = jnp.exp2((piece - high) * EXP_SCALE)
            if factor is not None:
                weight = weight * mult[factor]
            weights.append(weight)
        summed = functools.reduce(jnp.add, weights)
        summed = jnp.broadcast_to(jnp.sum(summed, axis=1, keepdims=True), summed.shape)
        weights = jnp.concatenate([w.astype(jnp.bfloat16) for w in weights], axis=1)
        if not first:
            summed = summed + tot[head] * fade
        tot[head] = summed
        if values_later:
            late[head] = weights
            acc[head] = acc[head] * fade
            return
        mixed = jnp.dot(weights, vbuf[slots, columns], preferred_element_type=jnp.float32)
        if not first:
            mixed = mixed + acc[head] * fade
        top[head] = high
        acc[head] = mixed

    def per_head(unroll, step_of):
        def body(index, carry):
            for u in range(unroll):
                step_of(index * unroll + u)
            return carry

        lax.fori_loop(0, HEADS // unroll, body, 0)

    def group(first_slot, factors, first, values_later, unroll):
        per_head(unroll, lambda head: head_group(head, first_slot, factors, first, values_later))

    def late_values(head, which, last):
        columns = pl.ds(pl.multiple_of(head * HEAD_DIM, HEAD_DIM), HEAD_DIM)
        mixed = acc[head] + jnp.dot(
            late[head, :, which * rows : (which + 1) * rows],
            vbuf[pl.ds((DG + which) * rows, rows), columns],
            preferred_element_type=jnp.float32,
        )
        if last:
            mixed_heads[:, columns] = (mixed / tot[head]).astype(mixed_heads.dtype)
        else:
            acc[head] = mixed

    for load in loads:
        load.wait()
    for kv in range(2):
        to_sib(kv).wait_recv()
    group(OWN, (None, None), True, False, 4)

    for kv in range(2):
        to_y(kv).wait_recv()

        @pl.when(has_p)
        def _():
            relay_y(kv).start()

        @pl.when(gives_y)
        def _():
            hand_y(kv, 0).start()
            hand_y(kv, 1).start()

        @pl.when(has_p)
        def _():
            to_zm(kv).wait_recv()
            relay_z(kv).start()

    @pl.when(has_m)
    def _():
        for kv in range(2):
            to_zp(kv).wait_recv()

    group(YN, (0, 1, 2), False, False, 4)

    def diagonal(kv):
        @pl.when(has_m)
        def _():
            relay_y(kv).wait_recv()

        @pl.when(has_m & gives_d)
        def _():
            hand_d(kv, 0).start()

        @pl.when(has_m)
        def _():
            relay_z(kv).wait_recv()

        @pl.when(has_m & gives_d)
        def _():
            hand_d(kv, 1).start()

    def handed(kv):
        @pl.when(x_valid)
        def _():
            hand_y(kv, 0).wait_recv()
            hand_y(kv, 1).wait_recv()

    diagonal(0)
    handed(0)
    group(DG, (3, 4), False, True, 4)
    load_w.wait()
    diagonal(1)
    per_head(HEADS, lambda head: late_values(head, 0, False))
    handed(1)
    per_head(HEADS, lambda head: late_values(head, 1, True))
    for n in range(0, wv.shape[1], 512):
        out[:, n : n + 512] = jnp.dot(
            mixed_heads[...], wv[:, n : n + 512], preferred_element_type=jnp.float32
        ).astype(out.dtype)

    for kv in range(2):
        to_sib(kv).wait_send()
        to_y(kv).wait_send()

        @pl.when(has_p)
        def _():
            to_zp(kv).wait_send()
            relay_y(kv).wait_send()
            relay_z(kv).wait_send()

        @pl.when(has_m)
        def _():
            to_zm(kv).wait_send()

        @pl.when(gives_y | has_m)
        def _():
            hand_y(kv, 0).wait_send()
            hand_y(kv, 1).wait_send()


def attention(devices, queries, keys, values, far_picks, out_weight):
    rows, width = queries.shape
    in_hbm = pl.BlockSpec(memory_space=pltpu.HBM)
    return pl.pallas_call(
        functools.partial(kernel, devices),
        out_shape=jax.ShapeDtypeStruct((rows, width), jnp.bfloat16),
        in_specs=[in_hbm] * 5,
        out_specs=pl.BlockSpec(memory_space=pltpu.VMEM),
        scratch_shapes=[
            pltpu.SMEM(far_picks.shape, jnp.int32),
            pltpu.VMEM((rows, width), jnp.bfloat16),
            pltpu.VMEM(out_weight.shape, jnp.bfloat16),
            pltpu.VMEM((HEADS, rows, 2 * rows), jnp.bfloat16),
            pltpu.VMEM((rows, width), jnp.bfloat16),
            pltpu.VMEM((7 * rows, width), jnp.bfloat16),
            pltpu.VMEM((7 * rows, width), jnp.bfloat16),
            pltpu.VMEM((5, rows, rows), jnp.float32),
            pltpu.VMEM((HEADS, rows, HEAD_DIM), jnp.float32),
            pltpu.VMEM((HEADS, rows, HEAD_DIM), jnp.float32),
            pltpu.VMEM((HEADS, rows, HEAD_DIM), jnp.float32),
            pltpu.SemaphoreType.DMA((5,)),
            pltpu.SemaphoreType.DMA((8, 2)),
            pltpu.SemaphoreType.DMA((8, 2)),
        ],
        compiler_params=pltpu.CompilerParams(
            collective_id=0, has_side_effects=True, vmem_limit_bytes=67_000_000
        ),
        name="relay_attention",
    )(far_picks, queries, keys, values, out_weight)


def solution(mesh):
    devices = mesh.shape["tm"]

    def body(queries, keys, values, far_picks, out_weight):
        return attention(devices, queries, keys, values, far_picks, out_weight)

    placed = (
        P(("vid", "tm"), None),
        P(("vid", "tm"), None),
        P(("vid", "tm"), None),
        P(("vid", "tm"), None),
        P(),
    )
    return jax.shard_map(
        body, mesh=mesh, in_specs=placed, out_specs=P(("vid", "tm"), None), check_vma=False
    )
```

```python
import functools
import math

import jax
import jax.numpy as jnp
from jax import lax
from jax.experimental import pallas as pl
from jax.experimental.pallas import tpu as pltpu
from jax.sharding import PartitionSpec as P

HEADS = 12
HEAD_DIM = 128
BLK = 64
NEG = -1e30
EXP_SCALE = HEAD_DIM ** (-0.5) * math.log2(math.e)
OWN, SIB, YN, ZP, ZM, DG, XF = range(7)
MESH = pl.DeviceIdType.MESH
PIECES = ({0: (0, 6), 2: (6, 12)}, {0: (0, 4), 1: (4, 6), 2: (6, 10), 3: (10, 12)})
BY_Y = ((0,), (0, 1))
BY_Z = ((2,), (2, 3))


def kernel(
    devices,
    picks_hbm,
    q_hbm,
    k_hbm,
    v_hbm,
    w_hbm,
    out,
    picks,
    qv,
    wv,
    late,
    mixed_heads,
    projected,
    kbuf,
    vbuf,
    mult,
    top,
    tot,
    acc,
    load_sem,
    send_sem,
    recv_sem,
):
    rows = q_hbm.shape[0]
    chips = devices // 2
    p = lax.axis_index("tm")
    chip = p // 2
    core = p % 2
    even = chip % 2 == 0
    step = jnp.where(even, 1, -1)
    has_p = (chip + 2 * step >= 0) & (chip + 2 * step < chips)
    has_m = (chip - 2 * step >= 0) & (chip - 2 * step < chips)
    gives_y = (core + chip) % 2 == 0
    gives_d = jnp.logical_not(gives_y)

    sib = p + 1 - 2 * core
    y_dev = p + 2 * step
    zp_dev = p + 4 * step
    zm_dev = p - 4 * step

    def slot(buf, index):
        return buf.at[pl.ds(index * rows, rows)]

    def part(kv, index, piece):
        first, end = PIECES[kv][piece]
        columns = pl.ds(first * HEAD_DIM, (end - first) * HEAD_DIM)
        return bufs[kv].at[pl.ds(index * rows, rows), columns]

    def remote(src, dst, number, kv, dev):
        return pltpu.make_async_remote_copy(
            src_ref=src,
            dst_ref=dst,
            send_sem=send_sem.at[number, kv],
            recv_sem=recv_sem.at[number, kv],
            device_id={"tm": dev},
            device_id_type=MESH,
        )

    bufs = (kbuf, vbuf)
    hbms = (k_hbm, v_hbm)

    def to_sib(kv):
        return remote(hbms[kv], slot(bufs[kv], SIB), 0, kv, sib)

    def to_y(kv):
        return remote(hbms[kv], slot(bufs[kv], YN), 1, kv, y_dev)

    def to_zp(kv):
        return remote(hbms[kv], slot(bufs[kv], ZM), 2, kv, zp_dev)

    def to_zm(kv):
        return remote(hbms[kv], slot(bufs[kv], ZP), 3, kv, zm_dev)

    def relay_y(kv, piece):
        return remote(part(kv, YN, piece), part(kv, DG, piece), 4 + piece, kv, zp_dev)

    def relay_z(kv, piece):
        return remote(part(kv, ZP, piece), part(kv, DG, piece), 4 + piece, kv, y_dev)

    def hand_y(kv, piece):
        return remote(part(kv, YN, piece), part(kv, XF, piece), 8 + piece, kv, sib)

    def hand_d(kv, piece):
        return remote(part(kv, DG, piece), part(kv, XF, piece), 8 + piece, kv, sib)

    load_w = pltpu.make_async_copy(w_hbm, wv, load_sem.at[4])
    load_picks = pltpu.make_async_copy(picks_hbm, picks, load_sem.at[3])
    load_picks.start()
    loads = [
        pltpu.make_async_copy(q_hbm, qv, load_sem.at[0]),
        pltpu.make_async_copy(k_hbm, slot(kbuf, OWN), load_sem.at[1]),
        pltpu.make_async_copy(v_hbm, slot(vbuf, OWN), load_sem.at[2]),
    ]
    for load in loads:
        load.start()

    barrier = pltpu.get_barrier_semaphore()

    def greet(dev):
        pl.semaphore_signal(barrier, inc=1, device_id={"tm": dev}, device_id_type=MESH)

    greet(sib)
    greet(y_dev)

    @pl.when(has_p)
    def _():
        greet(zp_dev)

    @pl.when(has_m)
    def _():
        greet(zm_dev)

    pl.semaphore_wait(barrier, 2 + jnp.where(has_p, 1, 0) + jnp.where(has_m, 1, 0))

    for kv in range(2):
        to_y(kv).start()

        @pl.when(has_p)
        def _():
            to_zp(kv).start()

        @pl.when(has_m)
        def _():
            to_zm(kv).start()

        to_sib(kv).start()

    load_w.start()
    load_picks.wait()

    ints = jnp.int32
    row_first = lax.broadcasted_iota(ints, (rows, rows), 0) < BLK
    col_first = lax.broadcasted_iota(ints, (rows, rows), 1) < BLK

    def fill(index, up, down, valid):
        one = jnp.where(valid, 1, 0)
        seconds = [
            jnp.where(even, picks[b, up] + picks[b, up + 1], picks[b, down] + picks[b, down + 1])
            for b in range(2)
        ]
        cells = [[((2 - n) * one).astype(jnp.float32), (n * one).astype(jnp.float32)] for n in seconds]
        mult[index] = jnp.where(
            row_first,
            jnp.where(col_first, cells[0][0], cells[0][1]),
            jnp.where(col_first, cells[1][0], cells[1][1]),
        )

    fill(0, 4, 0, True)
    fill(1, 6, 2, has_p)
    fill(2, 2, 6, has_m)
    fill(3, 0, 4, has_m)
    x_valid = gives_d | has_m
    mult[4] = jnp.full((rows, rows), jnp.where(x_valid, 1.0, 0.0), jnp.float32)

    @pl.when(jnp.logical_not(has_p))
    def _():
        vbuf[ZP * rows : (ZP + 1) * rows] = jnp.zeros((rows, vbuf.shape[1]), vbuf.dtype)

    @pl.when(jnp.logical_not(has_m))
    def _():
        vbuf[ZM * rows : (DG + 1) * rows] = jnp.zeros((2 * rows, vbuf.shape[1]), vbuf.dtype)

    @pl.when(jnp.logical_not(x_valid))
    def _():
        vbuf[XF * rows : (XF + 1) * rows] = jnp.zeros((rows, vbuf.shape[1]), vbuf.dtype)

    def head_group(head, first_slot, factors, first, values_later):
        columns = pl.ds(pl.multiple_of(head * HEAD_DIM, HEAD_DIM), HEAD_DIM)
        count = len(factors)
        slots = pl.ds(first_slot * rows, count * rows)
        scores = lax.dot_general(
            qv[:, columns],
            kbuf[slots, columns],
            (((1,), (1,)), ((), ())),
            preferred_element_type=jnp.float32,
        )
        pieces = []
        for i, factor in enumerate(factors):
            piece = scores[:, i * rows : (i + 1) * rows]
            if factor is not None:
                piece = jnp.where(mult[factor] > 0, piece, NEG)
            pieces.append(piece)
        high = functools.reduce(jnp.maximum, pieces)
        high = jnp.broadcast_to(jnp.max(high, axis=1, keepdims=True), high.shape)
        if not first:
            before = top[head]
            high = jnp.maximum(high, before)
            fade = jnp.exp2((before - high) * EXP_SCALE)
        weights = []
        for piece, factor in zip(pieces, factors):
            weight = jnp.exp2((piece - high) * EXP_SCALE)
            if factor is not None:
                weight = weight * mult[factor]
            weights.append(weight)
        summed = functools.reduce(jnp.add, weights)
        summed = jnp.broadcast_to(jnp.sum(summed, axis=1, keepdims=True), summed.shape)
        weights = jnp.concatenate([w.astype(jnp.bfloat16) for w in weights], axis=1)
        if not first:
            summed = summed + tot[head] * fade
        tot[head] = summed
        if values_later:
            late[head] = weights
            acc[head] = acc[head] * fade
            return
        mixed = jnp.dot(weights, vbuf[slots, columns], preferred_element_type=jnp.float32)
        if not first:
            mixed = mixed + acc[head] * fade
        top[head] = high
        acc[head] = mixed

    def per_head(unroll, step_of):
        def body(index, carry):
            for u in range(unroll):
                step_of(index * unroll + u)
            return carry

        lax.fori_loop(0, HEADS // unroll, body, 0)

    def group(first_slot, factors, first, values_later, unroll):
        per_head(unroll, lambda head: head_group(head, first_slot, factors, first, values_later))

    def late_values(head, which, last):
        columns = slice(head * HEAD_DIM, (head + 1) * HEAD_DIM)
        mixed = acc[head] + jnp.dot(
            late[head, :, which * rows : (which + 1) * rows],
            vbuf[pl.ds((DG + which) * rows, rows), columns],
            preferred_element_type=jnp.float32,
        )
        if last:
            mixed_heads[:, columns] = (mixed / tot[head]).astype(mixed_heads.dtype)
        else:
            acc[head] = mixed

    for load in loads:
        load.wait()
    for kv in range(2):
        to_sib(kv).wait_recv()
    group(OWN, (None, None), True, False, 4)

    for kv in range(2):
        to_y(kv).wait_recv()

        @pl.when(has_p)
        def _():
            for piece in BY_Y[kv]:
                relay_y(kv, piece).start()

        @pl.when(gives_y)
        def _():
            for piece in PIECES[kv]:
                hand_y(kv, piece).start()

        @pl.when(has_p)
        def _():
            to_zm(kv).wait_recv()
            for piece in BY_Z[kv]:
                relay_z(kv, piece).start()

    @pl.when(has_m)
    def _():
        for kv in range(2):
            to_zp(kv).wait_recv()

    group(YN, (0, 1, 2), False, False, 4)

    def diagonal(kv, piece):
        @pl.when(has_m)
        def _():
            relay_y(kv, piece).wait_recv()

        @pl.when(has_m & gives_d)
        def _():
            hand_d(kv, piece).start()

    def handed(kv, piece):
        @pl.when(x_valid)
        def _():
            hand_y(kv, piece).wait_recv()

    def heads_of(pieces):
        return [head for piece in pieces for head in range(*PIECES[1][piece])]

    def project(pieces):
        total = None
        for piece in pieces:
            first, end = PIECES[1][piece]
            columns = slice(first * HEAD_DIM, end * HEAD_DIM)
            term = jnp.dot(mixed_heads[:, columns], wv[columns, :], preferred_element_type=jnp.float32)
            total = term if total is None else total + term
        return total

    for piece in PIECES[0]:
        diagonal(0, piece)
    for piece in PIECES[0]:
        handed(0, piece)
    group(DG, (3, 4), False, True, 4)
    load_w.wait()
    early, final = (0, 2), (1, 3)
    for pieces in (early, final):
        for piece in pieces:
            diagonal(1, piece)
        for head in heads_of(pieces):
            late_values(head, 0, False)
    for pieces in (early, final):
        for piece in pieces:
            handed(1, piece)
        for head in heads_of(pieces):
            late_values(head, 1, True)
        if pieces is early:
            projected[...] = project(pieces)
        else:
            out[...] = (projected[...] + project(pieces)).astype(out.dtype)

    for kv in range(2):
        to_sib(kv).wait_send()
        to_y(kv).wait_send()

        @pl.when(has_p)
        def _():
            to_zp(kv).wait_send()
            for piece in BY_Y[kv]:
                relay_y(kv, piece).wait_send()
            for piece in BY_Z[kv]:
                relay_z(kv, piece).wait_send()

        @pl.when(has_m)
        def _():
            to_zm(kv).wait_send()

        @pl.when(gives_y | has_m)
        def _():
            for piece in PIECES[kv]:
                hand_y(kv, piece).wait_send()


def attention(devices, queries, keys, values, far_picks, out_weight):
    rows, width = queries.shape
    in_hbm = pl.BlockSpec(memory_space=pltpu.HBM)
    return pl.pallas_call(
        functools.partial(kernel, devices),
        out_shape=jax.ShapeDtypeStruct((rows, width), jnp.bfloat16),
        in_specs=[in_hbm] * 5,
        out_specs=pl.BlockSpec(memory_space=pltpu.VMEM),
        scratch_shapes=[
            pltpu.SMEM(far_picks.shape, jnp.int32),
            pltpu.VMEM((rows, width), jnp.bfloat16),
            pltpu.VMEM(out_weight.shape, jnp.bfloat16),
            pltpu.VMEM((HEADS, rows, 2 * rows), jnp.bfloat16),
            pltpu.VMEM((rows, width), jnp.bfloat16),
            pltpu.VMEM((rows, width), jnp.float32),
            pltpu.VMEM((7 * rows, width), jnp.bfloat16),
            pltpu.VMEM((7 * rows, width), jnp.bfloat16),
            pltpu.VMEM((5, rows, rows), jnp.float32),
            pltpu.VMEM((HEADS, rows, HEAD_DIM), jnp.float32),
            pltpu.VMEM((HEADS, rows, HEAD_DIM), jnp.float32),
            pltpu.VMEM((HEADS, rows, HEAD_DIM), jnp.float32),
            pltpu.SemaphoreType.DMA((5,)),
            pltpu.SemaphoreType.DMA((12, 2)),
            pltpu.SemaphoreType.DMA((12, 2)),
        ],
        compiler_params=pltpu.CompilerParams(
            collective_id=0, has_side_effects=True, vmem_limit_bytes=67_000_000
        ),
        name="relay_attention",
    )(far_picks, queries, keys, values, out_weight)


def solution(mesh):
    devices = mesh.shape["tm"]

    def body(queries, keys, values, far_picks, out_weight):
        return attention(devices, queries, keys, values, far_picks, out_weight)

    placed = (
        P(("vid", "tm"), None),
        P(("vid", "tm"), None),
        P(("vid", "tm"), None),
        P(("vid", "tm"), None),
        P(),
    )
    return jax.shard_map(
        body, mesh=mesh, in_specs=placed, out_specs=P(("vid", "tm"), None), check_vma=False
    )
```

```python
import functools
import math

import jax
import jax.numpy as jnp
from jax import lax
from jax.experimental import pallas as pl
from jax.experimental.pallas import tpu as pltpu
from jax.sharding import PartitionSpec as P

HEADS = 12
HEAD_DIM = 128
BLK = 64
NEG = -1e30
EXP_SCALE = HEAD_DIM ** (-0.5) * math.log2(math.e)
OWN, SIB, YN, ZP, ZM, DG, XF = range(7)
MESH = pl.DeviceIdType.MESH
PIECES = ({0: (0, 6), 2: (6, 12)}, {0: (0, 4), 1: (4, 6), 2: (6, 10), 3: (10, 12)})
BY_Y = ((0,), (0, 1))
BY_Z = ((2,), (2, 3))


def kernel(
    devices,
    picks_hbm,
    q_hbm,
    k_hbm,
    v_hbm,
    w_hbm,
    out,
    picks,
    qv,
    wv,
    late,
    mixed_heads,
    projected,
    kbuf,
    vbuf,
    mult,
    top,
    tot,
    acc,
    load_sem,
    send_sem,
    recv_sem,
):
    rows = q_hbm.shape[0]
    chips = devices // 2
    p = lax.axis_index("tm")
    chip = p // 2
    core = p % 2
    even = chip % 2 == 0
    step = jnp.where(even, 1, -1)
    has_p = (chip + 2 * step >= 0) & (chip + 2 * step < chips)
    has_m = (chip - 2 * step >= 0) & (chip - 2 * step < chips)
    gives_y = (core + chip) % 2 == 0
    gives_d = jnp.logical_not(gives_y)

    sib = p + 1 - 2 * core
    y_dev = p + 2 * step
    zp_dev = p + 4 * step
    zm_dev = p - 4 * step

    def slot(buf, index):
        return buf.at[pl.ds(index * rows, rows)]

    def part(kv, index, piece):
        first, end = PIECES[kv][piece]
        columns = pl.ds(first * HEAD_DIM, (end - first) * HEAD_DIM)
        return bufs[kv].at[pl.ds(index * rows, rows), columns]

    def remote(src, dst, number, kv, dev):
        return pltpu.make_async_remote_copy(
            src_ref=src,
            dst_ref=dst,
            send_sem=send_sem.at[number, kv],
            recv_sem=recv_sem.at[number, kv],
            device_id={"tm": dev},
            device_id_type=MESH,
        )

    bufs = (kbuf, vbuf)
    hbms = (k_hbm, v_hbm)

    def to_sib(kv):
        return remote(hbms[kv], slot(bufs[kv], SIB), 0, kv, sib)

    def to_y(kv):
        return remote(hbms[kv], slot(bufs[kv], YN), 1, kv, y_dev)

    def to_zp(kv):
        return remote(hbms[kv], slot(bufs[kv], ZM), 2, kv, zp_dev)

    def to_zm(kv):
        return remote(hbms[kv], slot(bufs[kv], ZP), 3, kv, zm_dev)

    def relay_y(kv, piece):
        return remote(part(kv, YN, piece), part(kv, DG, piece), 4 + piece, kv, zp_dev)

    def relay_z(kv, piece):
        return remote(part(kv, ZP, piece), part(kv, DG, piece), 4 + piece, kv, y_dev)

    def hand_y(kv, piece):
        return remote(part(kv, YN, piece), part(kv, XF, piece), 8 + piece, kv, sib)

    def hand_d(kv, piece):
        return remote(part(kv, DG, piece), part(kv, XF, piece), 8 + piece, kv, sib)

    load_w = pltpu.make_async_copy(w_hbm, wv, load_sem.at[4])
    load_picks = pltpu.make_async_copy(picks_hbm, picks, load_sem.at[3])
    load_picks.start()
    loads = [
        pltpu.make_async_copy(q_hbm, qv, load_sem.at[0]),
        pltpu.make_async_copy(k_hbm, slot(kbuf, OWN), load_sem.at[1]),
        pltpu.make_async_copy(v_hbm, slot(vbuf, OWN), load_sem.at[2]),
    ]
    for load in loads:
        load.start()

    barrier = pltpu.get_barrier_semaphore()

    def greet(dev):
        pl.semaphore_signal(barrier, inc=1, device_id={"tm": dev}, device_id_type=MESH)

    greet(sib)
    greet(y_dev)

    @pl.when(has_p)
    def _():
        greet(zp_dev)

    @pl.when(has_m)
    def _():
        greet(zm_dev)

    pl.semaphore_wait(barrier, 2 + jnp.where(has_p, 1, 0) + jnp.where(has_m, 1, 0))

    for kv in range(2):
        to_y(kv).start()

        @pl.when(has_p)
        def _():
            to_zp(kv).start()

        @pl.when(has_m)
        def _():
            to_zm(kv).start()

        to_sib(kv).start()

    load_w.start()
    load_picks.wait()

    ints = jnp.int32
    row_first = lax.broadcasted_iota(ints, (rows, rows), 0) < BLK
    col_first = lax.broadcasted_iota(ints, (rows, rows), 1) < BLK

    def fill(index, up, down, valid):
        one = jnp.where(valid, 1, 0)
        seconds = [
            jnp.where(even, picks[b, up] + picks[b, up + 1], picks[b, down] + picks[b, down + 1])
            for b in range(2)
        ]
        cells = [[((2 - n) * one).astype(jnp.float32), (n * one).astype(jnp.float32)] for n in seconds]
        mult[index] = jnp.where(
            row_first,
            jnp.where(col_first, cells[0][0], cells[0][1]),
            jnp.where(col_first, cells[1][0], cells[1][1]),
        )

    fill(0, 4, 0, True)
    fill(1, 6, 2, has_p)
    fill(2, 2, 6, has_m)
    fill(3, 0, 4, has_m)
    x_valid = gives_d | has_m
    mult[4] = jnp.full((rows, rows), jnp.where(x_valid, 1.0, 0.0), jnp.float32)

    @pl.when(jnp.logical_not(has_p))
    def _():
        vbuf[ZP * rows : (ZP + 1) * rows] = jnp.zeros((rows, vbuf.shape[1]), vbuf.dtype)

    @pl.when(jnp.logical_not(has_m))
    def _():
        vbuf[ZM * rows : (DG + 1) * rows] = jnp.zeros((2 * rows, vbuf.shape[1]), vbuf.dtype)

    @pl.when(jnp.logical_not(x_valid))
    def _():
        vbuf[XF * rows : (XF + 1) * rows] = jnp.zeros((rows, vbuf.shape[1]), vbuf.dtype)

    def head_group(head, first_slot, factors, first, values_later):
        columns = pl.ds(pl.multiple_of(head * HEAD_DIM, HEAD_DIM), HEAD_DIM)
        count = len(factors)
        slots = pl.ds(first_slot * rows, count * rows)
        scores = lax.dot_general(
            qv[:, columns],
            kbuf[slots, columns],
            (((1,), (1,)), ((), ())),
            preferred_element_type=jnp.float32,
        )
        pieces = []
        for i, factor in enumerate(factors):
            piece = scores[:, i * rows : (i + 1) * rows]
            if factor is not None:
                piece = jnp.where(mult[factor] > 0, piece, NEG)
            pieces.append(piece)
        high = functools.reduce(jnp.maximum, pieces)
        high = jnp.broadcast_to(jnp.max(high, axis=1, keepdims=True), high.shape)
        if not first:
            before = top[head]
            high = jnp.maximum(high, before)
            fade = jnp.exp2((before - high) * EXP_SCALE)
        weights = []
        for piece, factor in zip(pieces, factors):
            weight = jnp.exp2((piece - high) * EXP_SCALE)
            if factor is not None:
                weight = weight * mult[factor]
            weights.append(weight)
        summed = functools.reduce(jnp.add, weights)
        summed = jnp.broadcast_to(jnp.sum(summed, axis=1, keepdims=True), summed.shape)
        weights = jnp.concatenate([w.astype(jnp.bfloat16) for w in weights], axis=1)
        if not first:
            summed = summed + tot[head] * fade
        tot[head] = summed
        if values_later:
            late[head] = weights
            acc[head] = acc[head] * fade
            return
        mixed = jnp.dot(weights, vbuf[slots, columns], preferred_element_type=jnp.float32)
        if not first:
            mixed = mixed + acc[head] * fade
        top[head] = high
        acc[head] = mixed

    def per_head(unroll, step_of, first=0, end=HEADS):
        def body(index, carry):
            for u in range(unroll):
                step_of(index * unroll + u)
            return carry

        lax.fori_loop(first // unroll, end // unroll, body, 0)

    def group(first_slot, factors, first, values_later, unroll, start=0, end=HEADS):
        per_head(
            unroll,
            lambda head: head_group(head, first_slot, factors, first, values_later),
            start,
            end,
        )

    def late_values(head, which, last):
        columns = slice(head * HEAD_DIM, (head + 1) * HEAD_DIM)
        mixed = acc[head] + jnp.dot(
            late[head, :, which * rows : (which + 1) * rows],
            vbuf[pl.ds((DG + which) * rows, rows), columns],
            preferred_element_type=jnp.float32,
        )
        if last:
            mixed_heads[:, columns] = (mixed / tot[head]).astype(mixed_heads.dtype)
        else:
            acc[head] = mixed

    for load in loads:
        load.wait()
    for kv in range(2):
        to_sib(kv).wait_recv()
    group(OWN, (None, None), True, False, 4)

    for kv in range(2):
        to_y(kv).wait_recv()

        @pl.when(has_p & (gives_d | (kv == 0)))
        def _():
            for piece in BY_Y[kv]:
                relay_y(kv, piece).start()

        @pl.when(gives_y)
        def _():
            for piece in PIECES[kv]:
                hand_y(kv, piece).start()

        @pl.when(has_p)
        def _():
            to_zm(kv).wait_recv()

        @pl.when(has_p & (gives_y | (kv == 0)))
        def _():
            for piece in BY_Z[kv]:
                relay_z(kv, piece).start()

    @pl.when(has_m)
    def _():
        for kv in range(2):
            to_zp(kv).wait_recv()

    group(YN, (0, 1, 2), False, False, 4, 0, 4)

    @pl.when(has_p & gives_y)
    def _():
        for piece in BY_Y[1]:
            relay_y(1, piece).start()

    @pl.when(has_p & gives_d)
    def _():
        for piece in BY_Z[1]:
            relay_z(1, piece).start()

    group(YN, (0, 1, 2), False, False, 4, 4, HEADS)

    def diagonal(kv, piece):
        @pl.when(has_m)
        def _():
            relay_y(kv, piece).wait_recv()

        @pl.when(has_m & gives_d)
        def _():
            hand_d(kv, piece).start()

    def handed(kv, piece):
        @pl.when(x_valid)
        def _():
            hand_y(kv, piece).wait_recv()

    def heads_of(pieces):
        return [head for piece in pieces for head in range(*PIECES[1][piece])]

    def project(pieces):
        total = None
        for piece in pieces:
            first, end = PIECES[1][piece]
            columns = slice(first * HEAD_DIM, end * HEAD_DIM)
            term = jnp.dot(mixed_heads[:, columns], wv[columns, :], preferred_element_type=jnp.float32)
            total = term if total is None else total + term
        return total

    for piece in PIECES[0]:
        diagonal(0, piece)
    for piece in PIECES[0]:
        handed(0, piece)
    group(DG, (3, 4), False, True, 4)
    load_w.wait()
    early, final = (0, 2), (1, 3)
    for pieces in (early, final):
        for piece in pieces:
            diagonal(1, piece)
        for head in heads_of(pieces):
            late_values(head, 0, False)
    for pieces in (early, final):
        for piece in pieces:
            handed(1, piece)
        for head in heads_of(pieces):
            late_values(head, 1, True)
        if pieces is early:
            projected[...] = project(pieces)
        else:
            out[...] = (projected[...] + project(pieces)).astype(out.dtype)

    for kv in range(2):
        to_sib(kv).wait_send()
        to_y(kv).wait_send()

        @pl.when(has_p)
        def _():
            to_zp(kv).wait_send()
            for piece in BY_Y[kv]:
                relay_y(kv, piece).wait_send()
            for piece in BY_Z[kv]:
                relay_z(kv, piece).wait_send()

        @pl.when(has_m)
        def _():
            to_zm(kv).wait_send()

        @pl.when(gives_y | has_m)
        def _():
            for piece in PIECES[kv]:
                hand_y(kv, piece).wait_send()


def attention(devices, queries, keys, values, far_picks, out_weight):
    rows, width = queries.shape
    in_hbm = pl.BlockSpec(memory_space=pltpu.HBM)
    return pl.pallas_call(
        functools.partial(kernel, devices),
        out_shape=jax.ShapeDtypeStruct((rows, width), jnp.bfloat16),
        in_specs=[in_hbm] * 5,
        out_specs=pl.BlockSpec(memory_space=pltpu.VMEM),
        scratch_shapes=[
            pltpu.SMEM(far_picks.shape, jnp.int32),
            pltpu.VMEM((rows, width), jnp.bfloat16),
            pltpu.VMEM(out_weight.shape, jnp.bfloat16),
            pltpu.VMEM((HEADS, rows, 2 * rows), jnp.bfloat16),
            pltpu.VMEM((rows, width), jnp.bfloat16),
            pltpu.VMEM((rows, width), jnp.float32),
            pltpu.VMEM((7 * rows, width), jnp.bfloat16),
            pltpu.VMEM((7 * rows, width), jnp.bfloat16),
            pltpu.VMEM((5, rows, rows), jnp.float32),
            pltpu.VMEM((HEADS, rows, HEAD_DIM), jnp.float32),
            pltpu.VMEM((HEADS, rows, HEAD_DIM), jnp.float32),
            pltpu.VMEM((HEADS, rows, HEAD_DIM), jnp.float32),
            pltpu.SemaphoreType.DMA((5,)),
            pltpu.SemaphoreType.DMA((12, 2)),
            pltpu.SemaphoreType.DMA((12, 2)),
        ],
        compiler_params=pltpu.CompilerParams(
            collective_id=0, has_side_effects=True, vmem_limit_bytes=67_000_000
        ),
        name="relay_attention",
    )(far_picks, queries, keys, values, out_weight)


def solution(mesh):
    devices = mesh.shape["tm"]

    def body(queries, keys, values, far_picks, out_weight):
        return attention(devices, queries, keys, values, far_picks, out_weight)

    placed = (
        P(("vid", "tm"), None),
        P(("vid", "tm"), None),
        P(("vid", "tm"), None),
        P(("vid", "tm"), None),
        P(),
    )
    return jax.shard_map(
        body, mesh=mesh, in_specs=placed, out_specs=P(("vid", "tm"), None), check_vma=False
    )
```
